32 devices in a mesh: leaf: 8 (over z, y), grp: 4 (over x, core).
Axes of the slice: x: 2, y: 2, z: 4, core: 2. Of those that a mesh axis runs over, the one named last changes fastest.
Arguments:
- leaf_rhs: float32 [8, 8, 128, 512], P('leaf', 'grp'), may hold values from -6 to 6
- leaf_inv: float32 [8, 8, 128, 128], P('leaf', 'grp')
- coupling: float32 [8, 8, 128, 128], P('leaf', 'grp'), may hold values from -0.1875 to 0.1875
- pattern: int32 [8, 8], P('leaf', 'grp'), may hold values 0 or 1
- sep_rhs: float32 [8, 128, 512], P('leaf'), may hold values from -6 to 6
- sep_inv: float32 [8, 128, 128], P('leaf')
- chain_link: float32 [8, 128, 128], P('leaf'), may hold values from -0.4375 to 0.4375
Outputs:
- leaf_solution: float32 [8, 8, 128, 512], P('leaf', 'grp')
- sep_solution: float32 [8, 128, 512], P('leaf', None, 'grp')
The draws below stay inside these ranges and needn't reach their ends.
All inputs are finite; a program needn't handle non-finite values. No bound on the sum of `pattern` on one device may be relied on, other than what follows from the above.
Results may differ from the reference program's by a relative error of at most 0.0003.
Values sent between devices are 32-bit elements; how exact they have to be, the bound alone decides.
No kernel may reach another device: no remote copies, remote signals or barrier semaphores. Data moves between devices by JAX's collectives and lax.ppermute only.
A program may use at most 192 MiB of HBM per device.

```python
import jax
import jax.numpy as jnp
from jax import lax

W = 128
NRHS = 512
K = 8
NSEC = 8


def inverse_blocks(key, lead):
    key_diag = jax.random.fold_in(key, 11)
    key_off = jax.random.fold_in(key, 12)
    shape = lead + (W, W)
    diag_vals = jnp.exp(jax.random.uniform(key_diag, lead + (W,), jnp.float32, -0.7, 0.7))
    off = jax.random.normal(key_off, shape, jnp.float32) * (0.3 / jnp.sqrt(W * 1.0))
    eye = jnp.eye(W, dtype=jnp.float32)
    return off * (1.0 - eye) + eye * diag_vals[..., None, :]


def draw_leaf_inv(key, part):
    return inverse_blocks(key, (NSEC, K))


def draw_sep_inv(key, part):
    return inverse_blocks(key, (NSEC,))


def set_ends(array, own_key, least, top_value):
    longest = array.shape.index(max(array.shape))
    spots = []
    for shift in (0, 1):
        where = [jax.random.randint(jax.random.fold_in(own_key, axis), (), 0, length) for axis, length in enumerate(array.shape)]
        where[longest] = (where[longest] + shift) % array.shape[longest]
        spots.append(tuple(where))
    return array.at[spots[0]].set(least).at[spots[1]].set(top_value)


def steps_of(key, shape, split, least, top_value):
    factor_of = 1.0
    for position, shards_of in split:
        steps = jax.random.uniform(jax.random.fold_in(jax.random.fold_in(key, 6), position), (shards_of,), jnp.float32, least / len(split), top_value / len(split))
        factor_of = factor_of * jnp.repeat(jnp.exp(steps), shape[position] // shards_of).reshape((-1,) + (1,) * (len(shape) - 1 - position))
    return factor_of


def noise(key, dims, deviation, bound, split=(), kind=jnp.bfloat16):
    factor_of = steps_of(key, dims, split, -0.22, 0.18) if split else 1.0
    array = jax.random.normal(key, dims, jnp.float32) * deviation * factor_of
    return jnp.minimum(jnp.maximum(array, -bound), bound).astype(kind)


def setup_inputs(seed: int = 0) -> dict:
    streams_of = jax.random.split(jax.random.key(seed), 8)
    return {
        "leaf_rhs": noise(streams_of[0], (NSEC, K, W, NRHS), 1.0, 6.0, ((0, 8), (1, 4)), jnp.float32),
        "leaf_inv": draw_leaf_inv(jax.random.fold_in(streams_of[7], 71), 0),
        "coupling": noise(streams_of[2], (NSEC, K, W, W), (W * K) ** -0.5, 0.1875, ((0, 8), (1, 4)), jnp.float32),
        "pattern": set_ends((jax.random.randint(streams_of[3], (NSEC, K), 0, 4) < 3).astype(jnp.int32), jax.random.fold_in(streams_of[3], 1), 0, 1),
        "sep_rhs": noise(streams_of[4], (NSEC, W, NRHS), 1.0, 6.0, ((0, 8),), jnp.float32),
        "sep_inv": draw_sep_inv(jax.random.fold_in(streams_of[7], 71), 0),
        "chain_link": noise(streams_of[6], (NSEC, W, W), (W * 8 // 5) ** -0.5, 0.4375, ((0, 8),), jnp.float32),
    }


HIGH = lax.Precision.HIGHEST


def reference(leaf_rhs, leaf_inv, coupling, pattern, sep_rhs, sep_inv, chain_link):
    leaf_y = jnp.einsum("skij,skjr->skir", leaf_inv, leaf_rhs, precision=HIGH)
    present = pattern.astype(jnp.float32)[:, :, None, None]
    update = jnp.einsum("skij,skjr->sir", coupling * present, leaf_y, precision=HIGH)

    def forward_step(prev, items):
        inverse, link, rhs, upd = items
        inner = rhs - upd - jnp.matmul(link, prev, precision=HIGH)
        now = jnp.matmul(inverse, inner, precision=HIGH)
        return now, now

    start = jnp.zeros((W, NRHS), jnp.float32)
    _, sep_y = lax.scan(forward_step, start, (sep_inv, chain_link, sep_rhs, update))

    def backward_step(carried, items):
        inverse, link, value = items
        solved = jnp.matmul(inverse.T, value - carried, precision=HIGH)
        return jnp.matmul(link.T, solved, precision=HIGH), solved

    _, sep_solution = lax.scan(backward_step, start, (sep_inv, chain_link, sep_y), reverse=True)
    back = jnp.einsum("skji,sjr->skir", coupling, sep_solution, precision=HIGH)
    leaf_solution = jnp.einsum("skji,skjr->skir", leaf_inv, leaf_y - present * back, precision=HIGH)
    return leaf_solution, sep_solution
```

```python
import jax
import jax.numpy as jnp
from jax import lax
from jax.experimental import pallas as pl
from jax.experimental.pallas import tpu as pltpu
from jax.sharding import PartitionSpec as P

HIGH = lax.Precision.HIGHEST
F32 = jnp.float32
VMEM = pl.BlockSpec(memory_space=pltpu.VMEM)
SMEM = pl.BlockSpec(memory_space=pltpu.SMEM)


def dot(a, b):
    return jnp.dot(a, b, precision=HIGH, preferred_element_type=F32)


def dot_ta(a, b):
    return lax.dot_general(
        a, b, (((0,), (0,)), ((), ())), precision=HIGH, preferred_element_type=F32
    )


def dot_tb(a, b):
    return lax.dot_general(
        a, b, (((1,), (1,)), ((), ())), precision=HIGH, preferred_element_type=F32
    )


def shaped(*shape):
    return jax.ShapeDtypeStruct(shape, F32)


def call(body, outs, flops, moved, *args):
    return pl.pallas_call(
        body,
        out_shape=outs,
        in_specs=[SMEM if a.dtype == jnp.int32 else VMEM for a in args],
        out_specs=jax.tree.map(lambda _: VMEM, outs),
        cost_estimate=pl.CostEstimate(flops=flops, bytes_accessed=moved, transcendentals=0),
        compiler_params=pltpu.CompilerParams(vmem_limit_bytes=48 << 20),
    )(*args)


def map_rows(place, inverse, link, out):
    rows = out.shape[0]
    start = pl.multiple_of(place[1] * rows, rows)
    out[...] = -dot(inverse[0, pl.ds(start, rows), :], link[0])


def partial_sums(place, pattern, rhs, leaf_inv, coupling, inverse, kept, sent, down):
    count, order = down.shape[0], down.shape[1]
    groups = kept.shape[0] * 2
    for k in range(count):
        present = pattern[0, k].astype(F32)
        mixed = dot(coupling[0, k] * present, leaf_inv[0, k])
        down[k] = dot(inverse[0], mixed)
    width = kept.shape[2]
    for slot in range(groups):
        start = pl.multiple_of((place[1] ^ slot) * width, width)
        total = dot(down[0], rhs[0, 0, :, pl.ds(start, width)])
        for k in range(1, count):
            total += dot(down[k], rhs[0, k, :, pl.ds(start, width)])
        (sent if slot % 2 else kept)[slot // 2] = total


def leaf_base(rhs, leaf_inv, base):
    for k in range(base.shape[0]):
        base[k] = dot_ta(leaf_inv[0, k], dot(leaf_inv[0, k], rhs[0, k]))


def own_columns(place, rhs, inverse, out):
    width = out.shape[1]
    start = pl.multiple_of(place[1] * width, width)
    out[...] = dot(inverse[0], rhs[0, :, pl.ds(start, width)])


def operator_row(place, maps, row, held):
    groups, sections, rows, order = maps.shape
    me, mine = place[0], place[1]
    diagonal = (
        lax.broadcasted_iota(jnp.int32, (order, order), 0)
        == lax.broadcasted_iota(jnp.int32, (order, order), 1)
    ).astype(F32)

    def slot_of(quarter):
        far = quarter ^ mine
        index, bit, low = 0, groups // 2, 1
        while bit:
            index = index + (far // bit) % 2 * low
            bit, low = bit // 2, low * 2
        return index

    def load(section):
        return jnp.concatenate(
            [maps[slot_of(q), section ^ me] for q in range(groups)], axis=0
        )

    held[0] = diagonal * (me == 0).astype(F32)

    @pl.loop(1, sections, unroll=sections <= 8)
    def _(section):
        reached = dot_tb(held[section - 1], load(section))
        held[section] = reached + diagonal * (me == section).astype(F32)

    row[sections - 1] = held[sections - 1]

    @pl.loop(0, sections - 1, unroll=sections <= 8)
    def _(turn):
        section = sections - 2 - turn
        row[section] = held[section] + dot(row[section + 1], load(section + 1))


def apply_row(row, offsets, out):
    total = dot(row[0], offsets[0])
    for section in range(1, row.shape[0]):
        total += dot(row[section], offsets[section])
    out[...] = total


def finish(place, base, down, inverse, spread, leaves, solved):
    groups, width = spread.shape[0], spread.shape[2]
    for j in range(groups):
        for k in range(base.shape[0]):
            cols = slice(j * width, (j + 1) * width)
            leaves[0, k, :, cols] = base[k, :, cols] - dot_ta(down[k], spread[j])
    solved[0] = dot_ta(inverse[0], spread[place[1]])


def swap(value, axis, bit):
    count = lax.axis_size(axis)
    return lax.ppermute(value, axis, [(i, i ^ bit) for i in range(count)])


def shards(leaf_rhs, leaf_inv, coupling, pattern, sep_rhs, sep_inv, chain_link):
    sections, groups = lax.axis_size("leaf"), lax.axis_size("grp")
    count, order, columns = leaf_rhs.shape[1:]
    width = columns // groups
    place = jnp.stack([lax.axis_index("leaf"), lax.axis_index("grp")]).astype(jnp.int32)
    cube = 2 * order**3

    maps = call(
        map_rows, shaped(order // groups, order), cube // groups, 3 * order * order * 4,
        place, sep_inv, chain_link,
    )[None]
    bit = 1
    while bit < sections:
        maps = jnp.concatenate([maps, swap(maps, "leaf", bit)], axis=0)
        bit *= 2
    maps = maps[None]
    bit = groups // 2
    while bit:
        maps = jnp.concatenate([maps, swap(maps, "grp", bit)], axis=0)
        bit //= 2
    row = pl.pallas_call(
        operator_row,
        out_shape=shaped(sections, order, order),
        in_specs=[SMEM, VMEM],
        out_specs=VMEM,
        scratch_shapes=[pltpu.VMEM((sections, order, order), F32)],
        cost_estimate=pl.CostEstimate(
            flops=2 * sections * cube, bytes_accessed=2 * maps.size * 4, transcendentals=0
        ),
        compiler_params=pltpu.CompilerParams(vmem_limit_bytes=48 << 20),
    )(place, maps)

    half = shaped(groups // 2, order, width)
    kept, sent, down = call(
        partial_sums,
        (half, half, shaped(count, order, order)),
        (2 * count + groups * count) * cube,
        3 * leaf_rhs.size * 4,
        place, pattern, leaf_rhs, leaf_inv, coupling, sep_inv,
    )
    own = call(
        own_columns, shaped(order, width), cube, 3 * order * order * 4, place, sep_rhs, sep_inv
    )
    bit = 1
    while bit < groups:
        total = kept + swap(sent, "grp", bit)
        kept, sent = total[0::2], total[1::2]
        bit *= 2
    offset = own - total[0]
    offsets = lax.all_to_all(
        jnp.broadcast_to(offset, (sections, order, width)), "leaf", 0, 0, tiled=True
    )
    base = call(
        leaf_base, shaped(count, order, columns), 8 * count * cube, 3 * leaf_rhs.size * 4,
        leaf_rhs, leaf_inv,
    )
    carried = call(
        apply_row, shaped(order, width), sections * cube, 2 * row.size * 4, row, offsets
    )
    spread = lax.all_gather(carried, "grp")
    return call(
        finish,
        (shaped(1, count, order, columns), shaped(1, order, width)),
        (4 * count + 1) * cube,
        3 * leaf_rhs.size * 4,
        place, base, down, sep_inv, spread,
    )


def solution(mesh):
    in_specs = (
        P("leaf", "grp", None, None),
        P("leaf", "grp", None, None),
        P("leaf", "grp", None, None),
        P("leaf", "grp"),
        P("leaf", None, None),
        P("leaf", None, None),
        P("leaf", None, None),
    )
    out_specs = (P("leaf", "grp", None, None), P("leaf", None, "grp"))
    return jax.shard_map(shards, mesh=mesh, in_specs=in_specs, out_specs=out_specs, check_vma=False)
```

```python
import jax
import jax.numpy as jnp
from jax import lax
from jax.experimental import pallas as pl
from jax.experimental.pallas import tpu as pltpu
from jax.sharding import PartitionSpec as P

HIGH = lax.Precision.HIGHEST
F32 = jnp.float32
VMEM = pl.BlockSpec(memory_space=pltpu.VMEM)
HBM = pl.BlockSpec(memory_space=pltpu.HBM)


def dot(a, b):
    return jnp.dot(a, b, precision=HIGH, preferred_element_type=F32)


def dot_ta(a, b):
    return lax.dot_general(
        a, b, (((0,), (0,)), ((), ())), precision=HIGH, preferred_element_type=F32
    )


def dot_tb(a, b):
    return lax.dot_general(
        a, b, (((1,), (1,)), ((), ())), precision=HIGH, preferred_element_type=F32
    )


def shaped(*shape):
    return jax.ShapeDtypeStruct(shape, F32)


def call(body, outs, flops, moved, *args, held=(), far=0):
    args = [pltpu.with_memory_space_constraint(a, pltpu.HBM) for a in args[:far]] + list(args[far:])
    return pl.pallas_call(
        body,
        out_shape=outs,
        in_specs=[HBM] * far + [VMEM] * (len(args) - far),
        out_specs=jax.tree.map(lambda _: VMEM, outs),
        scratch_shapes=held,
        cost_estimate=pl.CostEstimate(flops=flops, bytes_accessed=moved, transcendentals=0),
        compiler_params=pltpu.CompilerParams(vmem_limit_bytes=48 << 20),
    )(*args)


def landing(args):
    holds = [
        (pltpu.SMEM if a.dtype == jnp.int32 else pltpu.VMEM)(a.shape, a.dtype) for a in args
    ]
    return holds + [pltpu.SemaphoreType.DMA((len(args),))]


def fetch(sources, targets, sems):
    copies = [
        pltpu.make_async_copy(a, b, sems.at[i]) for i, (a, b) in enumerate(zip(sources, targets))
    ]
    for copy in copies:
        copy.start()
    return copies


def begin(*refs):
    sources, (maps, kept, sent, down) = refs[:6], refs[6:10]
    targets, sems = refs[10:16], refs[16]
    inverse, link, pattern, leaf_inv, coupling, rhs = targets
    copies = fetch(sources, targets, sems)
    group = lax.axis_index("grp")
    count, order = down.shape[0], down.shape[1]
    groups, width, rows = kept.shape[0] * 2, kept.shape[2], maps.shape[0]
    copies[0].wait()
    copies[1].wait()
    start = pl.multiple_of(group * rows, rows)
    maps[...] = -dot(inverse[0, pl.ds(start, rows), :], link[0])
    for copy in copies[2:5]:
        copy.wait()
    for k in range(count):
        present = pattern[0, k].astype(F32)
        mixed = dot(coupling[0, k] * present, leaf_inv[0, k])
        down[k] = dot(inverse[0], mixed)
    copies[5].wait()
    for slot in range(groups):
        start = pl.multiple_of((group ^ slot) * width, width)
        total = dot(down[0], rhs[0, 0, :, pl.ds(start, width)])
        for k in range(1, count):
            total += dot(down[k], rhs[0, k, :, pl.ds(start, width)])
        (sent if slot % 2 else kept)[slot // 2] = total


def leaf_base(rhs_far, inv_far, base, rhs, leaf_inv, sems):
    copies = fetch((rhs_far, inv_far), (rhs, leaf_inv), sems)
    for copy in copies:
        copy.wait()
    for k in range(base.shape[0]):
        base[k] = dot_ta(leaf_inv[0, k], dot(leaf_inv[0, k], rhs[0, k]))


def own_columns(rhs_far, inverse_far, out, rhs, inverse, sems):
    width = out.shape[1]
    start = pl.multiple_of(lax.axis_index("grp") * width, width)
    copies = fetch((rhs_far, inverse_far), (rhs, inverse), sems)
    for copy in copies:
        copy.wait()
    out[...] = dot(inverse[0], rhs[0, :, pl.ds(start, width)])


def operator_row(maps, row, held):
    groups, sections, rows, order = maps.shape
    me, mine = lax.axis_index("leaf"), lax.axis_index("grp")
    diagonal = (
        lax.broadcasted_iota(jnp.int32, (order, order), 0)
        == lax.broadcasted_iota(jnp.int32, (order, order), 1)
    ).astype(F32)

    def slot_of(far, size):
        index, bit, low = 0, size // 2, 1
        while bit:
            index = index + (far // bit) % 2 * low
            bit, low = bit // 2, low * 2
        return index

    def load(section):
        spot = slot_of(section ^ me, sections)
        return jnp.concatenate(
            [maps[slot_of(q ^ mine, groups), spot] for q in range(groups)], axis=0
        )

    held[0] = diagonal * (me == 0).astype(F32)

    @pl.loop(1, sections, unroll=sections <= 8)
    def _(section):
        reached = dot_tb(held[section - 1], load(section))
        held[section] = reached + diagonal * (me == section).astype(F32)

    row[sections - 1] = held[sections - 1]

    @pl.loop(0, sections - 1, unroll=sections <= 8)
    def _(turn):
        section = sections - 2 - turn
        row[section] = held[section] + dot(row[section + 1], load(section + 1))


def apply_row(row, offsets, out):
    total = dot(row[0], offsets[0])
    for section in range(1, row.shape[0]):
        total += dot(row[section], offsets[section])
    out[...] = total


def finish(base, down, inverse, spread, leaves, solved):
    groups, width = spread.shape[0], spread.shape[2]
    for j in range(groups):
        for k in range(base.shape[0]):
            cols = slice(j * width, (j + 1) * width)
            leaves[0, k, :, cols] = base[k, :, cols] - dot_ta(down[k], spread[j])
    solved[0] = dot_ta(inverse[0], spread[lax.axis_index("grp")])


def swap(value, axis, bit):
    count = lax.axis_size(axis)
    return lax.ppermute(value, axis, [(i, i ^ bit) for i in range(count)])


def shards(leaf_rhs, leaf_inv, coupling, pattern, sep_rhs, sep_inv, chain_link):
    sections, groups = lax.axis_size("leaf"), lax.axis_size("grp")
    count, order, columns = leaf_rhs.shape[1:]
    width = columns // groups
    cube = 2 * order**3

    half = shaped(groups // 2, order, width)
    first = (sep_inv, chain_link, pattern, leaf_inv, coupling, leaf_rhs)
    maps, kept, sent, down = call(
        begin,
        (shaped(order // groups, order), half, half, shaped(count, order, order)),
        (2 * count + groups * count + 1) * cube,
        2 * leaf_rhs.size * 4,
        *first, held=landing(first), far=6,
    )
    maps = maps[None]
    rounds = [("leaf", 2**i) for i in reversed(range((sections - 1).bit_length()))]

    own = call(
        own_columns, shaped(order, width), cube, 3 * order * order * 4, sep_rhs, sep_inv,
        held=landing((sep_rhs, sep_inv)), far=2,
    )
    bit = 1
    while bit < groups:
        total = kept + swap(sent, "grp", bit)
        kept, sent = total[0::2], total[1::2]
        bit *= 2
    offset = own - total[0]

    for axis, bit in rounds[:-1]:
        maps = jnp.concatenate([maps, swap(maps, axis, bit)], axis=0)
    maps, offset = lax.optimization_barrier((maps, offset))
    for axis, bit in rounds[-1:]:
        maps = jnp.concatenate([maps, swap(maps, axis, bit)], axis=0)
    maps = maps[None]
    bit = groups // 2
    while bit:
        maps = jnp.concatenate([maps, swap(maps, "grp", bit)], axis=0)
        bit //= 2
    row = call(
        operator_row, shaped(sections, order, order), 2 * sections * cube, 2 * maps.size * 4,
        maps, held=[pltpu.VMEM((sections, order, order), F32)],
    )

    offsets = lax.all_to_all(
        jnp.broadcast_to(offset, (sections, order, width)), "leaf", 0, 0, tiled=True
    )
    base = call(
        leaf_base, shaped(count, order, columns), 8 * count * cube, 3 * leaf_rhs.size * 4,
        leaf_rhs, leaf_inv, held=landing((leaf_rhs, leaf_inv)), far=2,
    )
    carried = call(
        apply_row, shaped(order, width), sections * cube, 2 * row.size * 4, row, offsets
    )
    spread = lax.all_gather(carried, "grp")
    return call(
        finish,
        (shaped(1, count, order, columns), shaped(1, order, width)),
        (4 * count + 1) * cube,
        3 * leaf_rhs.size * 4,
        base, down, sep_inv, spread,
    )


def solution(mesh):
    in_specs = (
        P("leaf", "grp", None, None),
        P("leaf", "grp", None, None),
        P("leaf", "grp", None, None),
        P("leaf", "grp"),
        P("leaf", None, None),
        P("leaf", None, None),
        P("leaf", None, None),
    )
    out_specs = (P("leaf", "grp", None, None), P("leaf", None, "grp"))
    return jax.shard_map(shards, mesh=mesh, in_specs=in_specs, out_specs=out_specs, check_vma=False)
```

```python
import jax
import jax.numpy as jnp
from jax import lax
from jax.experimental import pallas as pl
from jax.experimental.pallas import tpu as pltpu
from jax.sharding import PartitionSpec as P

HIGH = lax.Precision.HIGHEST
F32 = jnp.float32
VMEM = pl.BlockSpec(memory_space=pltpu.VMEM)
HBM = pl.BlockSpec(memory_space=pltpu.HBM)


def dot(a, b):
    return jnp.dot(a, b, precision=HIGH, preferred_element_type=F32)


def dot_ta(a, b):
    return lax.dot_general(
        a, b, (((0,), (0,)), ((), ())), precision=HIGH, preferred_element_type=F32
    )


def dot_tb(a, b):
    return lax.dot_general(
        a, b, (((1,), (1,)), ((), ())), precision=HIGH, preferred_element_type=F32
    )


def shaped(*shape):
    return jax.ShapeDtypeStruct(shape, F32)


def call(body, outs, flops, moved, *args, held=(), far=0, out_specs=None):
    args = [pltpu.with_memory_space_constraint(a, pltpu.HBM) for a in args[:far]] + list(args[far:])
    return pl.pallas_call(
        body,
        out_shape=outs,
        in_specs=[HBM] * far + [VMEM] * (len(args) - far),
        out_specs=out_specs or jax.tree.map(lambda _: VMEM, outs),
        scratch_shapes=held,
        cost_estimate=pl.CostEstimate(flops=flops, bytes_accessed=moved, transcendentals=0),
        compiler_params=pltpu.CompilerParams(vmem_limit_bytes=48 << 20),
    )(*args)


def landing(*args):
    holds = [
        (pltpu.SMEM if a.dtype == jnp.int32 else pltpu.VMEM)(a.shape, a.dtype) for a in args
    ]
    return holds + [pltpu.SemaphoreType.DMA((len(args),))]


def fetch(sources, targets, sems):
    copies = [
        pltpu.make_async_copy(a, b, sems.at[i]) for i, (a, b) in enumerate(zip(sources, targets))
    ]
    for copy in copies:
        copy.start()
    return copies


def columns_of(block, width):
    return pl.ds(pl.multiple_of(block * width, width), width)


def map_half(inverse_far, link_far, out, inverse, link, sems):
    copies = fetch((inverse_far, link_far), (inverse, link), sems)
    rows = out.shape[1]
    start = pl.multiple_of((lax.axis_index("grp") & 1) * rows, rows)
    for copy in copies:
        copy.wait()
    out[0] = -dot(inverse[0, pl.ds(start, rows), :], link[0])


def begin(*refs):
    sources, outs = refs[:5], refs[5:-6]
    down, slots = outs[0], outs[1:]
    targets, sems = refs[-6:-1], refs[-1]
    inverse, pattern, leaf_inv, coupling, rhs = targets
    copies = fetch(sources, targets, sems)
    group = lax.axis_index("grp")
    count, width = down.shape[0], slots[0].shape[1]
    for copy in copies[:4]:
        copy.wait()
    for k in range(count):
        present = pattern[0, k].astype(F32)
        mixed = dot(coupling[0, k] * present, leaf_inv[0, k])
        down[k] = dot(inverse[0], mixed)
    copies[4].wait()
    for slot in reversed(range(len(slots))):
        cols = columns_of(group ^ slot, width)
        total = dot(down[0], rhs[0, 0, :, cols])
        for k in range(1, count):
            total += dot(down[k], rhs[0, k, :, cols])
        slots[slot][...] = total


def leaf_base(rhs_far, inv_far, base, rhs, leaf_inv, sems):
    copies = fetch((rhs_far, inv_far), (rhs, leaf_inv), sems)
    for copy in copies:
        copy.wait()
    for k in range(base.shape[0]):
        base[k] = dot_ta(leaf_inv[0, k], dot(leaf_inv[0, k], rhs[0, k]))


def own_columns(rhs_far, inverse_far, out, rhs, inverse, sems):
    copies = fetch((rhs_far, inverse_far), (rhs, inverse), sems)
    for copy in copies:
        copy.wait()
    out[...] = dot(inverse[0], rhs[0, :, columns_of(lax.axis_index("grp"), out.shape[1])])


def operator_rows(mine, mine_rest, other, other_rest, held, maps):
    sections, both, order = held.shape
    rows = order // 2
    me, half = lax.axis_index("leaf"), lax.axis_index("grp") & 1
    near = pl.ds(pl.multiple_of(half * rows, rows), rows)
    rest = pl.ds(pl.multiple_of((1 - half) * rows, rows), rows)

    @pl.loop(0, sections // 2, unroll=sections <= 8)
    def _(i):
        maps[2 * i ^ me, near] = mine[i]
        maps[2 * i ^ me, rest] = mine_rest[i]
        maps[2 * i ^ 1 ^ me, near] = other[i]
        maps[2 * i ^ 1 ^ me, rest] = other_rest[i]

    line = lax.broadcasted_iota(jnp.int32, (both, order), 0)
    column = lax.broadcasted_iota(jnp.int32, (both, order), 1)
    target = jnp.where(line < order, me, me ^ 1)
    ones = jnp.where((line & (order - 1)) == column, target, -1)

    held[0] = (ones == 0).astype(F32)

    @pl.loop(1, sections, unroll=sections <= 8)
    def _(section):
        held[section] = dot_tb(held[section - 1], maps[section]) + (ones == section).astype(F32)

    @pl.loop(0, sections - 1, unroll=sections <= 8)
    def _(turn):
        section = sections - 2 - turn
        held[section] += dot(held[section + 1], maps[section + 1])


def apply_rows(which, *refs):
    held, parts, out = refs[0], refs[1:-1], refs[-1]
    order = held.shape[2]
    rows = slice(which * order, (which + 1) * order)
    me = lax.axis_index("leaf")
    size = parts[0].shape[0]
    total = None
    for p, part in enumerate(parts):
        for i in range(size):
            piece = dot(held[2 * (p * size + i) ^ me, rows], part[i])
            total = piece if total is None else total + piece
    out[...] = total


def leaf_piece(slot, base, down, carried, out):
    width = out.shape[2]
    for k in range(out.shape[0]):
        cols = columns_of(lax.axis_index("grp") ^ slot, width)
        out[k] = base[k, :, cols] - dot_ta(down[k], carried[...])


def own_piece(inverse_far, base, down, carried, out, solved, inverse, sems):
    copies = fetch((inverse_far,), (inverse,), sems)
    leaf_piece(0, base, down, carried, out)
    copies[0].wait()
    solved[0] = dot_ta(inverse[0], carried[...])


def last_piece(*refs):
    (base, down, carried), done = refs[:3], refs[3:-3]
    leaves, piece, sems = refs[-3:]
    width = piece.shape[2]
    group, slot = lax.axis_index("grp"), len(done)

    def put(i, source):
        target = leaves.at[0, :, :, columns_of(group ^ i, width)]
        return pltpu.make_async_copy(source, target, sems.at[i])

    copies = [put(i, source) for i, source in enumerate(done)]
    for copy in copies:
        copy.start()
    leaf_piece(slot, base, down, carried, piece)
    copies.append(put(slot, piece))
    copies[slot].start()
    for copy in copies:
        copy.wait()


def swap(value, axis, bit):
    count = lax.axis_size(axis)
    return lax.ppermute(value, axis, [(i, i ^ bit) for i in range(count)])


def gather_pairs(value):
    bit, sections = 2, lax.axis_size("leaf")
    parts = [value]
    while bit < sections:
        if len(parts) > 1:
            value = jnp.concatenate(parts, axis=0)
        masks = [bit] if 2 * bit >= sections else [bit, 2 * bit, 3 * bit]
        parts = [value] + [swap(value, "leaf", m) for m in masks]
        bit *= 4 if len(masks) > 1 else 2
    return parts


def after(value, *others):
    return lax.optimization_barrier((value,) + others)[0]


def shards(leaf_rhs, leaf_inv, coupling, pattern, sep_rhs, sep_inv, chain_link):
    sections, groups = lax.axis_size("leaf"), lax.axis_size("grp")
    count, order, columns = leaf_rhs.shape[1:]
    width = columns // groups
    cube = 2 * order**3
    block = shaped(order, width)
    block_bytes = order * width * 4

    half = call(
        map_half, shaped(1, order // 2, order), cube // 2, 3 * block_bytes,
        sep_inv, chain_link, held=landing(sep_inv, chain_link), far=2,
    )
    map_parts = gather_pairs(half)

    first = (sep_inv, pattern, leaf_inv, coupling, leaf_rhs)
    down, *slots = call(
        begin,
        (shaped(count, order, order),) + (block,) * groups,
        (2 * count + groups * count) * cube,
        2 * leaf_rhs.size * 4,
        *first, held=landing(*first), far=5,
    )
    slots = dict(enumerate(slots))
    bit = 1
    while bit < groups:
        arrived = {m: swap(slots[m + bit], "grp", bit) for m in reversed(range(0, groups, 2 * bit))}
        if 2 * bit == groups:
            own = call(
                own_columns, block, cube, 3 * block_bytes, sep_rhs, sep_inv,
                held=landing(sep_rhs, sep_inv), far=2,
            )
            slots[0] = own - slots[0]
            offset = slots[0] - arrived[0]
        else:
            slots = {m: slots[m] + arrived[m] for m in arrived}
        bit *= 2

    mine = jnp.concatenate(map_parts, axis=0)
    mine_rest = swap(mine, "grp", 1)
    other = swap(mine, "leaf", 1)
    other_rest = swap(other, "grp", 1)
    rows = call(
        operator_rows, shaped(sections, 2 * order, order), 4 * sections * cube,
        4 * sections * block_bytes, mine, mine_rest, other, other_rest,
        held=[pltpu.VMEM((sections, order, order), F32)],
    )

    base = call(
        leaf_base, shaped(count, order, columns), 8 * count * cube, 3 * leaf_rhs.size * 4,
        leaf_rhs, leaf_inv, held=landing(leaf_rhs, leaf_inv), far=2,
    )

    offsets = gather_pairs(offset[None])

    def applied(which):
        return call(
            lambda *refs: apply_rows(which, *refs), block, sections // 2 * cube,
            sections * block_bytes, rows, *offsets,
        )

    theirs = applied(1)
    carried = {0: swap(theirs, "leaf", 1)}
    carried[0] = applied(0) + carried[0]

    for m in range(1, groups):
        low = m & -m
        carried[m] = swap(carried[m ^ low], "grp", low)
    piece = shaped(count, order, width)
    own_leaves, solved = call(
        own_piece, (piece, shaped(1, order, width)), (count + 1) * cube, 6 * block_bytes,
        sep_inv, base, down, carried[0], held=landing(sep_inv), far=1,
    )
    done = [own_leaves]
    for m in range(1, groups - 1):
        done.append(
            call(
                lambda *refs, m=m: leaf_piece(m, *refs), piece, count * cube, 6 * block_bytes,
                base, down, carried[m],
            )
        )
    leaves = call(
        last_piece, shaped(1, count, order, columns), count * cube,
        2 * leaf_rhs.size * 4, base, down, carried[groups - 1], *done,
        held=[pltpu.VMEM((count, order, width), F32), pltpu.SemaphoreType.DMA((groups,))],
        out_specs=HBM,
    )
    return leaves, solved


def solution(mesh):
    in_specs = (
        P("leaf", "grp", None, None),
        P("leaf", "grp", None, None),
        P("leaf", "grp", None, None),
        P("leaf", "grp"),
        P("leaf", None, None),
        P("leaf", None, None),
        P("leaf", None, None),
    )
    out_specs = (P("leaf", "grp", None, None), P("leaf", None, "grp"))
    return jax.shard_map(shards, mesh=mesh, in_specs=in_specs, out_specs=out_specs, check_vma=False)
```

```python
import jax
import jax.numpy as jnp
from jax import lax
from jax.experimental import pallas as pl
from jax.experimental.pallas import tpu as pltpu
from jax.sharding import PartitionSpec as P

HIGH = lax.Precision.HIGHEST
F32 = jnp.float32
BF16 = jnp.bfloat16
VMEM = pl.BlockSpec(memory_space=pltpu.VMEM)
HBM = pl.BlockSpec(memory_space=pltpu.HBM)


def dot(a, b):
    return jnp.dot(a, b, precision=HIGH, preferred_element_type=F32)


def dot_ta(a, b):
    return lax.dot_general(
        a, b, (((0,), (0,)), ((), ())), precision=HIGH, preferred_element_type=F32
    )


def split(x):
    high = x.astype(BF16)
    return high, (x - high.astype(F32)).astype(BF16)


def left(x):
    high, low = split(x)
    return jnp.concatenate([high, low, high], axis=1)


def right(x, axis=0):
    high, low = split(x)
    return jnp.concatenate([high, high, low], axis=axis)


def dot3(a, b):
    return jnp.dot(left(a), right(b), preferred_element_type=F32)


def dot3_tb(a, b):
    return lax.dot_general(
        left(a), right(b, 1), (((1,), (1,)), ((), ())), preferred_element_type=F32
    )


def shaped(*shape):
    return jax.ShapeDtypeStruct(shape, F32)


def call(body, outs, flops, moved, *args, held=(), far=0, out_specs=None):
    args = [pltpu.with_memory_space_constraint(a, pltpu.HBM) for a in args[:far]] + list(args[far:])
    return pl.pallas_call(
        body,
        out_shape=outs,
        in_specs=[HBM] * far + [VMEM] * (len(args) - far),
        out_specs=out_specs or jax.tree.map(lambda _: VMEM, outs),
        scratch_shapes=held,
        cost_estimate=pl.CostEstimate(flops=flops, bytes_accessed=moved, transcendentals=0),
        compiler_params=pltpu.CompilerParams(vmem_limit_bytes=48 << 20),
    )(*args)


def landing(*args):
    holds = [
        (pltpu.SMEM if a.dtype == jnp.int32 else pltpu.VMEM)(a.shape, a.dtype) for a in args
    ]
    return holds + [pltpu.SemaphoreType.DMA((len(args),))]


def fetch(sources, targets, sems):
    copies = [
        pltpu.make_async_copy(a, b, sems.at[i]) for i, (a, b) in enumerate(zip(sources, targets))
    ]
    for copy in copies:
        copy.start()
    return copies


def columns_of(block, width):
    return pl.ds(pl.multiple_of(block * width, width), width)


def begin(*refs):
    sources, outs = refs[:5], refs[5:-6]
    down, slots = outs[0], outs[1:]
    targets, sems = refs[-6:-1], refs[-1]
    inverse, pattern, leaf_inv, coupling, rhs = targets
    copies = fetch(sources, targets, sems)
    group = lax.axis_index("grp")
    count, width = down.shape[0], slots[0].shape[1]
    for copy in copies[:4]:
        copy.wait()
    for k in range(count):
        present = pattern[0, k].astype(F32)
        mixed = dot(coupling[0, k] * present, leaf_inv[0, k])
        down[k] = dot(inverse[0], mixed)
    copies[4].wait()
    for slot in reversed(range(len(slots))):
        cols = columns_of(group ^ slot, width)
        total = dot(down[0], rhs[0, 0, :, cols])
        for k in range(1, count):
            total += dot(down[k], rhs[0, k, :, cols])
        slots[slot][...] = total


def section_map(inverse, link, order_only, out):
    out[0] = -dot(inverse[0], link[0])


def leaf_base(rhs, leaf_inv, down, base, factors):
    order = down.shape[1]
    for k in range(base.shape[0]):
        gram = dot_ta(leaf_inv[0, k], leaf_inv[0, k])
        base[k] = dot(gram, rhs[0, k])
        factors[k * order : (k + 1) * order] = left(down[k].T)


def own_columns(rhs, inverse, out):
    out[...] = dot(inverse[0], rhs[0, :, columns_of(lax.axis_index("grp"), out.shape[1])])


def operator_rows(*refs):
    parts, (held, maps) = refs[:-2], refs[-2:]
    sections, both, order = held.shape
    me = lax.axis_index("leaf")
    size = parts[0].shape[0]
    half = len(parts) // 2

    @pl.loop(0, size, unroll=size <= 8)
    def _(i):
        for p in range(half):
            maps[2 * (p * size + i) ^ me] = parts[p][i]
            maps[2 * (p * size + i) ^ 1 ^ me] = parts[half + p][i]

    line = lax.broadcasted_iota(jnp.int32, (both, order), 0)
    column = lax.broadcasted_iota(jnp.int32, (both, order), 1)
    target = jnp.where(line < order, me, me ^ 1)
    ones = jnp.where((line & (order - 1)) == column, target, -1)

    held[0] = (ones == 0).astype(F32)

    @pl.loop(1, sections, unroll=sections <= 8)
    def _(section):
        held[section] = dot3_tb(held[section - 1], maps[section]) + (ones == section).astype(F32)

    @pl.loop(0, sections - 1, unroll=sections <= 8)
    def _(turn):
        section = sections - 2 - turn
        held[section] += dot3(held[section + 1], maps[section + 1])


def apply_rows(which, *refs):
    held, parts, out = refs[0], refs[1:-1], refs[-1]
    order = held.shape[2]
    rows = slice(which * order, (which + 1) * order)
    me = lax.axis_index("leaf")
    size = parts[0].shape[0]
    total = None
    for p, part in enumerate(parts):
        for i in range(size):
            piece = dot(held[2 * (p * size + i) ^ me, rows], part[i])
            total = piece if total is None else total + piece
    out[...] = total


def finish(base, factors, inverse, spread, leaves, solved, pieces, sems):
    groups, count, order, width = pieces.shape
    copies = []
    for j in range(groups):
        cols = slice(j * width, (j + 1) * width)
        taken = jnp.dot(factors[...], right(spread[j]), preferred_element_type=F32)
        for k in range(count):
            pieces[j, k] = base[k, :, cols] - taken[k * order : (k + 1) * order]
        copy = pltpu.make_async_copy(pieces.at[j], leaves.at[0, :, :, cols], sems.at[j])
        copy.start()
        copies.append(copy)
    solved[0] = dot_ta(inverse[0], spread[lax.axis_index("grp")])
    for copy in copies:
        copy.wait()


def swap(value, axis, bit):
    count = lax.axis_size(axis)
    return lax.ppermute(value, axis, [(i, i ^ bit) for i in range(count)])


def gather_pairs(value):
    bit, sections = 2, lax.axis_size("leaf")
    parts = [value]
    while bit < sections:
        if len(parts) > 1:
            value = jnp.concatenate(parts, axis=0)
        masks = [bit] if 2 * bit >= sections else [bit, 2 * bit, 3 * bit]
        parts = [value] + [swap(value, "leaf", m) for m in masks]
        bit *= 4 if len(masks) > 1 else 2
    return parts


def shards(leaf_rhs, leaf_inv, coupling, pattern, sep_rhs, sep_inv, chain_link):
    sections, groups = lax.axis_size("leaf"), lax.axis_size("grp")
    count, order, columns = leaf_rhs.shape[1:]
    width = columns // groups
    cube = 2 * order**3
    block = shaped(order, width)
    block_bytes = order * width * 4

    first = (sep_inv, pattern, leaf_inv, coupling, leaf_rhs)
    down, *slots = call(
        begin,
        (shaped(count, order, order),) + (block,) * groups,
        (2 * count + groups * count) * cube,
        2 * leaf_rhs.size * 4,
        *first, held=landing(*first), far=5,
    )
    step = call(
        section_map, shaped(1, order, order), cube, 3 * block_bytes,
        sep_inv, chain_link, down,
    )
    slots = dict(enumerate(slots))
    own = call(own_columns, block, cube, 3 * block_bytes, sep_rhs, sep_inv)
    bit = 1
    while bit < groups:
        ahead = {
            m: slots[m] + swap(slots[m + bit], "grp", bit)
            for m in reversed(range(2 * bit, groups, 2 * bit))
        }
        slots = {0: slots[0] + swap(slots[bit], "grp", bit), **ahead}
        bit *= 2
    maps = gather_pairs(step)
    others = [swap(part, "leaf", 1) for part in maps]
    offset = own - slots[0]
    offsets = gather_pairs(offset[None])
    rows = call(
        operator_rows, shaped(sections, 2 * order, order), 4 * sections * cube,
        4 * sections * block_bytes, *maps, *others,
        held=[pltpu.VMEM((sections, order, order), F32)],
    )

    base, factors = call(
        leaf_base,
        (shaped(count, order, columns), jax.ShapeDtypeStruct((count * order, 3 * order), BF16)),
        (groups + 1) * count * cube, 3 * leaf_rhs.size * 4, leaf_rhs, leaf_inv, down,
    )

    def applied(which):
        return call(
            lambda *refs: apply_rows(which, *refs), block, sections // 2 * cube,
            sections * block_bytes, rows, *offsets,
        )

    theirs = swap(applied(1), "leaf", 1)
    carried = applied(0) + theirs
    spread = lax.all_gather(carried, "grp")
    return call(
        finish, (shaped(1, count, order, columns), shaped(1, order, width)),
        (4 * count + 1) * cube, 3 * leaf_rhs.size * 4,
        base, factors, sep_inv, spread,
        held=[pltpu.VMEM((groups, count, order, width), F32), pltpu.SemaphoreType.DMA((groups,))],
        out_specs=(HBM, VMEM),
    )


def solution(mesh):
    in_specs = (
        P("leaf", "grp", None, None),
        P("leaf", "grp", None, None),
        P("leaf", "grp", None, None),
        P("leaf", "grp"),
        P("leaf", None, None),
        P("leaf", None, None),
        P("leaf", None, None),
    )
    out_specs = (P("leaf", "grp", None, None), P("leaf", None, "grp"))
    return jax.shard_map(shards, mesh=mesh, in_specs=in_specs, out_specs=out_specs, check_vma=False)
```

```python
import jax
import jax.numpy as jnp
from jax import lax
from jax.experimental import pallas as pl
from jax.experimental.pallas import tpu as pltpu
from jax.sharding import PartitionSpec as P

HIGH = lax.Precision.HIGHEST
F32 = jnp.float32
BF16 = jnp.bfloat16
VMEM = pl.BlockSpec(memory_space=pltpu.VMEM)
HBM = pl.BlockSpec(memory_space=pltpu.HBM)


def dot(a, b):
    return jnp.dot(a, b, precision=HIGH, preferred_element_type=F32)


def dot_ta(a, b):
    return lax.dot_general(
        a, b, (((0,), (0,)), ((), ())), precision=HIGH, preferred_element_type=F32
    )


def split(x):
    high = x.astype(BF16)
    return high, (x - high.astype(F32)).astype(BF16)


def left(x):
    high, low = split(x)
    return jnp.concatenate([high, low, high], axis=1)


def right(x, axis=0):
    high, low = split(x)
    return jnp.concatenate([high, high, low], axis=axis)


def dot3(a, b):
    return jnp.dot(left(a), right(b), preferred_element_type=F32)


def dot3_tb(a, b):
    return lax.dot_general(
        left(a), right(b, 1), (((1,), (1,)), ((), ())), preferred_element_type=F32
    )


def shaped(*shape):
    return jax.ShapeDtypeStruct(shape, F32)


def call(body, outs, flops, moved, *args, held=(), far=0, out_specs=None):
    args = [pltpu.with_memory_space_constraint(a, pltpu.HBM) for a in args[:far]] + list(args[far:])
    return pl.pallas_call(
        body,
        out_shape=outs,
        in_specs=[HBM] * far + [VMEM] * (len(args) - far),
        out_specs=out_specs or jax.tree.map(lambda _: VMEM, outs),
        scratch_shapes=held,
        cost_estimate=pl.CostEstimate(flops=flops, bytes_accessed=moved, transcendentals=0),
        compiler_params=pltpu.CompilerParams(vmem_limit_bytes=48 << 20),
    )(*args)


def landing(*args):
    holds = [
        (pltpu.SMEM if a.dtype == jnp.int32 else pltpu.VMEM)(a.shape, a.dtype) for a in args
    ]
    return holds + [pltpu.SemaphoreType.DMA((len(args),))]


def fetch(sources, targets, sems):
    copies = [
        pltpu.make_async_copy(a, b, sems.at[i]) for i, (a, b) in enumerate(zip(sources, targets))
    ]
    for copy in copies:
        copy.start()
    return copies


def columns_of(block, width):
    return pl.ds(pl.multiple_of(block * width, width), width)


def begin(*refs):
    sources, outs = refs[:5], refs[5:-6]
    down, slots = outs[0], outs[1:]
    targets, sems = refs[-6:-1], refs[-1]
    inverse, pattern, leaf_inv, coupling, rhs = targets
    copies = fetch(sources, targets, sems)
    group = lax.axis_index("grp")
    count, width = down.shape[0], slots[0].shape[1]
    for copy in copies[:4]:
        copy.wait()
    for k in range(count):
        present = pattern[0, k].astype(F32)
        mixed = dot(coupling[0, k] * present, leaf_inv[0, k])
        down[k] = dot(inverse[0], mixed)
    copies[4].wait()
    joined = left(jnp.concatenate([down[k] for k in range(count)], axis=1))
    for first in reversed(range(0, len(slots), 2)):
        pair = [columns_of(group ^ slot, width) for slot in range(first, first + 2)]
        stacked = jnp.concatenate(
            [jnp.concatenate([rhs[0, k, :, cols] for cols in pair], axis=1) for k in range(count)],
            axis=0,
        )
        total = jnp.dot(joined, right(stacked), preferred_element_type=F32)
        slots[first][...] = total[:, :width]
        slots[first + 1][...] = total[:, width:]


def section_map(inverse, link, order_only, out):
    out[0] = -dot(inverse[0], link[0])


def leaf_base(rhs, leaf_inv, down, base, factors):
    order = down.shape[1]
    for k in range(base.shape[0]):
        gram = dot_ta(leaf_inv[0, k], leaf_inv[0, k])
        base[k] = dot(gram, rhs[0, k])
        factors[k * order : (k + 1) * order] = left(down[k].T)


def own_columns(rhs, inverse, out):
    out[...] = dot(inverse[0], rhs[0, :, columns_of(lax.axis_index("grp"), out.shape[1])])


def operator_rows(*refs):
    parts, (held, maps) = refs[:-2], refs[-2:]
    sections, both, order = held.shape
    me = lax.axis_index("leaf")
    at = 0
    for part in parts:
        size, begun = part.shape[0], at

        @pl.loop(0, size, unroll=size <= 8)
        def _(i):
            spot = i + begun
            maps[(2 * spot if begun < sections // 2 else 2 * spot + 1 - sections) ^ me] = part[i]

        at += size

    line = lax.broadcasted_iota(jnp.int32, (both, order), 0)
    column = lax.broadcasted_iota(jnp.int32, (both, order), 1)
    target = jnp.where(line < order, me, me ^ 1)
    ones = jnp.where((line & (order - 1)) == column, target, -1)

    held[0] = (ones == 0).astype(F32)

    @pl.loop(1, sections, unroll=sections <= 8)
    def _(section):
        held[section] = dot3_tb(held[section - 1], maps[section]) + (ones == section).astype(F32)

    @pl.loop(0, sections - 1, unroll=sections <= 8)
    def _(turn):
        section = sections - 2 - turn
        held[section] += dot3(held[section + 1], maps[section + 1])


def apply_rows(which, held, order_only, *refs):
    parts, out = refs[:-1], refs[-1]
    order = held.shape[2]
    rows = slice(which * order, (which + 1) * order)
    me = lax.axis_index("leaf")
    size = parts[0].shape[0]
    total = None
    for p, part in enumerate(parts):
        for i in range(size):
            piece = dot(held[2 * (p * size + i) ^ me, rows], part[i])
            total = piece if total is None else total + piece
    out[...] = total


def leaf_blocks(slots, base, factors, spread, out):
    count, order = base.shape[:2]
    width = spread.shape[2]
    for first in range(0, len(slots), 2):
        ready = range(first, min(first + 2, len(slots)))
        stacked = jnp.concatenate([spread[i] for i in ready], axis=1)
        taken = jnp.dot(factors[...], right(stacked), preferred_element_type=F32)
        for i in ready:
            cols = columns_of(lax.axis_index("grp") ^ slots[i], width)
            near = slice((i - first) * width, (i - first + 1) * width)
            for k in range(count):
                out[i, k] = base[k, :, cols] - taken[k * order : (k + 1) * order, near]


def early_blocks(slots, base, factors, inverse, spread, out, solved):
    leaf_blocks(slots, base, factors, spread, out)
    solved[0] = dot_ta(inverse[0], spread[0])


def late_blocks(early, late, base, factors, spread, done, leaves, fresh, sems):
    width = spread.shape[2]

    def put(i, slot, source):
        target = leaves.at[0, :, :, columns_of(lax.axis_index("grp") ^ slot, width)]
        return pltpu.make_async_copy(source, target, sems.at[i])

    copies = [put(i, slot, done.at[i]) for i, slot in enumerate(early)]
    for copy in copies:
        copy.start()
    leaf_blocks(late, base, factors, spread, fresh)
    for i, slot in enumerate(late):
        copies.append(put(len(early) + i, slot, fresh.at[i]))
        copies[-1].start()
    for copy in copies:
        copy.wait()


def swap(value, axis, bit):
    count = lax.axis_size(axis)
    return lax.ppermute(value, axis, [(i, i ^ bit) for i in range(count)])


def gather_pairs(value):
    bit, sections = 2, lax.axis_size("leaf")
    parts = [value]
    while bit < sections:
        if len(parts) > 1:
            value = jnp.concatenate(parts, axis=0)
        masks = [bit] if 2 * bit >= sections else [bit, 2 * bit, 3 * bit]
        parts = [value] + [swap(value, "leaf", m) for m in masks]
        bit *= 4 if len(masks) > 1 else 2
    return parts


def shards(leaf_rhs, leaf_inv, coupling, pattern, sep_rhs, sep_inv, chain_link):
    sections, groups = lax.axis_size("leaf"), lax.axis_size("grp")
    count, order, columns = leaf_rhs.shape[1:]
    width = columns // groups
    cube = 2 * order**3
    block = shaped(order, width)
    block_bytes = order * width * 4

    first = (sep_inv, pattern, leaf_inv, coupling, leaf_rhs)
    down, *slots = call(
        begin,
        (shaped(count, order, order),) + (block,) * groups,
        (2 * count + groups * count) * cube,
        2 * leaf_rhs.size * 4,
        *first, held=landing(*first), far=5,
    )
    step = call(
        section_map, shaped(1, order, order), cube, 3 * block_bytes,
        sep_inv, chain_link, down,
    )
    slots = dict(enumerate(slots))
    own = call(own_columns, block, cube, 3 * block_bytes, sep_rhs, sep_inv)
    bit = 1
    while bit < groups:
        ahead = {
            m: slots[m] + swap(slots[m + bit], "grp", bit)
            for m in reversed(range(2 * bit, groups, 2 * bit))
        }
        slots = {0: slots[0] + swap(slots[bit], "grp", bit), **ahead}
        bit *= 2
    maps = gather_pairs(step)
    middle = len(maps) // 2
    others = [
        swap(jnp.concatenate(pair, axis=0), "leaf", 1) for pair in (maps[:middle], maps[middle:]) if pair
    ]
    offset = own - slots[0]
    offsets = gather_pairs(offset[None])
    rows = call(
        operator_rows, shaped(sections, 2 * order, order), 4 * sections * cube,
        4 * sections * block_bytes, *maps, *others,
        held=[pltpu.VMEM((sections, order, order), F32)],
    )

    base, factors = call(
        leaf_base,
        (shaped(count, order, columns), jax.ShapeDtypeStruct((count * order, 3 * order), BF16)),
        (groups + 1) * count * cube, 3 * leaf_rhs.size * 4, leaf_rhs, leaf_inv, down,
    )

    def applied(which, order_only):
        return call(
            lambda *refs: apply_rows(which, *refs), block, sections // 2 * cube,
            sections * block_bytes, rows, order_only, *offsets,
        )

    theirs = swap(applied(1, down), "leaf", 1)
    carried = applied(0, factors) + theirs
    spread, slots, bit = carried[None], [0], groups // 2
    while bit > 1:
        spread = jnp.concatenate([spread, swap(spread, "grp", bit)], axis=0)
        slots = slots + [slot ^ bit for slot in slots]
        bit //= 2
    late = [slot ^ 1 for slot in slots]
    arrived = swap(spread, "grp", 1)
    done, solved = call(
        lambda *refs: early_blocks(slots, *refs),
        (shaped(len(slots), count, order, width), shaped(1, order, width)),
        (len(slots) * count + 1) * cube, 4 * leaf_rhs.size, base, factors, sep_inv, spread,
    )
    leaves = call(
        lambda *refs: late_blocks(slots, late, *refs), shaped(1, count, order, columns),
        len(late) * count * cube, 8 * leaf_rhs.size, base, factors, arrived, done,
        held=[
            pltpu.VMEM((len(late), count, order, width), F32),
            pltpu.SemaphoreType.DMA((groups,)),
        ],
        out_specs=HBM,
    )
    return leaves, solved


def solution(mesh):
    in_specs = (
        P("leaf", "grp", None, None),
        P("leaf", "grp", None, None),
        P("leaf", "grp", None, None),
        P("leaf", "grp"),
        P("leaf", None, None),
        P("leaf", None, None),
        P("leaf", None, None),
    )
    out_specs = (P("leaf", "grp", None, None), P("leaf", None, "grp"))
    return jax.shard_map(shards, mesh=mesh, in_specs=in_specs, out_specs=out_specs, check_vma=False)
```

```python
import jax
import jax.numpy as jnp
from jax import lax
from jax.experimental import pallas as pl
from jax.experimental.pallas import tpu as pltpu
from jax.sharding import PartitionSpec as P

HIGH = lax.Precision.HIGHEST
F32 = jnp.float32
BF16 = jnp.bfloat16
VMEM = pl.BlockSpec(memory_space=pltpu.VMEM)
HBM = pl.BlockSpec(memory_space=pltpu.HBM)


def dot(a, b):
    return jnp.dot(a, b, precision=HIGH, preferred_element_type=F32)


def dot_ta(a, b):
    return lax.dot_general(
        a, b, (((0,), (0,)), ((), ())), precision=HIGH, preferred_element_type=F32
    )


def split(x):
    high = x.astype(BF16)
    return high, (x - high.astype(F32)).astype(BF16)


def left(x):
    high, low = split(x)
    return jnp.concatenate([high, low, high], axis=1)


def right(x, axis=0):
    high, low = split(x)
    return jnp.concatenate([high, high, low], axis=axis)


def dot3(a, b):
    return jnp.dot(left(a), right(b), preferred_element_type=F32)


def dot3_tb(a, b):
    return lax.dot_general(
        left(a), right(b, 1), (((1,), (1,)), ((), ())), preferred_element_type=F32
    )


def shaped(*shape):
    return jax.ShapeDtypeStruct(shape, F32)


def call(body, outs, flops, moved, *args, held=(), far=0, out_specs=None):
    args = [pltpu.with_memory_space_constraint(a, pltpu.HBM) for a in args[:far]] + list(args[far:])
    return pl.pallas_call(
        body,
        out_shape=outs,
        in_specs=[HBM] * far + [VMEM] * (len(args) - far),
        out_specs=out_specs or jax.tree.map(lambda _: VMEM, outs),
        scratch_shapes=held,
        cost_estimate=pl.CostEstimate(flops=flops, bytes_accessed=moved, transcendentals=0),
        compiler_params=pltpu.CompilerParams(vmem_limit_bytes=48 << 20),
    )(*args)


def landing(*args):
    holds = [
        (pltpu.SMEM if a.dtype == jnp.int32 else pltpu.VMEM)(a.shape, a.dtype) for a in args
    ]
    return holds + [pltpu.SemaphoreType.DMA((len(args),))]


def fetch(sources, targets, sems):
    copies = [
        pltpu.make_async_copy(a, b, sems.at[i]) for i, (a, b) in enumerate(zip(sources, targets))
    ]
    for copy in copies:
        copy.start()
    return copies


def columns_of(block, width):
    return pl.ds(pl.multiple_of(block * width, width), width)


def begin(*refs):
    sources, outs = refs[:5], refs[5:-6]
    down, slots = outs[0], outs[1:]
    targets, sems = refs[-6:-1], refs[-1]
    inverse, pattern, leaf_inv, coupling, rhs = targets
    copies = fetch(sources, targets, sems)
    group = lax.axis_index("grp")
    count, width = down.shape[0], slots[0].shape[1]
    for copy in copies[:4]:
        copy.wait()
    for k in range(count):
        present = pattern[0, k].astype(F32)
        mixed = dot3(coupling[0, k] * present, leaf_inv[0, k])
        down[k] = dot3(inverse[0], mixed)
    copies[4].wait()
    joined = left(jnp.concatenate([down[k] for k in range(count)], axis=1))
    for first in reversed(range(0, len(slots), 2)):
        pair = [columns_of(group ^ slot, width) for slot in range(first, first + 2)]
        stacked = jnp.concatenate(
            [jnp.concatenate([rhs[0, k, :, cols] for cols in pair], axis=1) for k in range(count)],
            axis=0,
        )
        total = jnp.dot(joined, right(stacked), preferred_element_type=F32)
        slots[first][...] = total[:, :width]
        slots[first + 1][...] = total[:, width:]


def section_map(inverse, link, order_only, out):
    out[0] = -dot(inverse[0], link[0])


def leaf_base(rhs, leaf_inv, down, base, factors):
    order = down.shape[1]
    for k in range(base.shape[0]):
        gram = dot_ta(leaf_inv[0, k], leaf_inv[0, k])
        base[k] = dot(gram, rhs[0, k])
        factors[k * order : (k + 1) * order] = left(down[k].T)


def own_columns(rhs, inverse, out):
    out[...] = dot(inverse[0], rhs[0, :, columns_of(lax.axis_index("grp"), out.shape[1])])


def operator_rows(*refs):
    parts, (held, maps) = refs[:-2], refs[-2:]
    sections, both, order = held.shape
    me = lax.axis_index("leaf")
    at = 0
    for part in parts:
        size, begun = part.shape[0], at

        @pl.loop(0, size, unroll=size <= 8)
        def _(i):
            spot = i + begun
            maps[(2 * spot if begun < sections // 2 else 2 * spot + 1 - sections) ^ me] = part[i]

        at += size

    line = lax.broadcasted_iota(jnp.int32, (both, order), 0)
    column = lax.broadcasted_iota(jnp.int32, (both, order), 1)
    target = jnp.where(line < order, me, me ^ 1)
    ones = jnp.where((line & (order - 1)) == column, target, -1)

    held[0] = (ones == 0).astype(F32)

    @pl.loop(1, sections, unroll=sections <= 8)
    def _(section):
        held[section] = dot3_tb(held[section - 1], maps[section]) + (ones == section).astype(F32)

    @pl.loop(0, sections - 1, unroll=sections <= 8)
    def _(turn):
        section = sections - 2 - turn
        held[section] += dot3(held[section + 1], maps[section + 1])


def apply_rows(which, held, order_only, *refs):
    parts, out = refs[:-1], refs[-1]
    order = held.shape[2]
    rows = slice(which * order, (which + 1) * order)
    me = lax.axis_index("leaf")
    size = parts[0].shape[0]
    total = None
    for p, part in enumerate(parts):
        for i in range(size):
            piece = dot(held[2 * (p * size + i) ^ me, rows], part[i])
            total = piece if total is None else total + piece
    out[...] = total


def leaf_blocks(slots, base, factors, spread, out):
    count, order = base.shape[:2]
    width = spread.shape[2]
    for first in range(0, len(slots), 2):
        ready = range(first, min(first + 2, len(slots)))
        stacked = jnp.concatenate([spread[i] for i in ready], axis=1)
        taken = jnp.dot(factors[...], right(stacked), preferred_element_type=F32)
        for i in ready:
            cols = columns_of(lax.axis_index("grp") ^ slots[i], width)
            near = slice((i - first) * width, (i - first + 1) * width)
            for k in range(count):
                out[i, k] = base[k, :, cols] - taken[k * order : (k + 1) * order, near]


def early_blocks(slots, base, factors, inverse, spread, out, solved):
    leaf_blocks(slots, base, factors, spread, out)
    solved[0] = dot_ta(inverse[0], spread[0])


def late_blocks(early, late, base, factors, spread, done, leaves, fresh, sems):
    width = spread.shape[2]

    def put(i, slot, source):
        target = leaves.at[0, :, :, columns_of(lax.axis_index("grp") ^ slot, width)]
        return pltpu.make_async_copy(source, target, sems.at[i])

    copies = [put(i, slot, done.at[i]) for i, slot in enumerate(early)]
    for copy in copies:
        copy.start()
    leaf_blocks(late, base, factors, spread, fresh)
    for i, slot in enumerate(late):
        copies.append(put(len(early) + i, slot, fresh.at[i]))
        copies[-1].start()
    for copy in copies:
        copy.wait()


def swap(value, axis, bit):
    count = lax.axis_size(axis)
    return lax.ppermute(value, axis, [(i, i ^ bit) for i in range(count)])


def gather_pairs(value):
    bit, sections = 2, lax.axis_size("leaf")
    parts = [value]
    while bit < sections:
        if len(parts) > 1:
            value = jnp.concatenate(parts, axis=0)
        masks = [bit] if 2 * bit >= sections else [bit, 2 * bit, 3 * bit]
        parts = [value] + [swap(value, "leaf", m) for m in masks]
        bit *= 4 if len(masks) > 1 else 2
    return parts


def shards(leaf_rhs, leaf_inv, coupling, pattern, sep_rhs, sep_inv, chain_link):
    sections, groups = lax.axis_size("leaf"), lax.axis_size("grp")
    count, order, columns = leaf_rhs.shape[1:]
    width = columns // groups
    cube = 2 * order**3
    block = shaped(order, width)
    block_bytes = order * width * 4
    placed = (40 * sections * cube, 60 << 20)

    first = (sep_inv, pattern, leaf_inv, coupling, leaf_rhs)
    down, *slots = call(
        begin,
        (shaped(count, order, order),) + (block,) * groups,
        *placed,
        *first, held=landing(*first), far=5,
    )
    step = call(
        section_map, shaped(1, order, order), *placed,
        sep_inv, chain_link, down,
    )
    slots = dict(enumerate(slots))
    own = call(own_columns, block, *placed, sep_rhs, sep_inv)
    bit = 1
    while bit < groups:
        ahead = {
            m: slots[m] + swap(slots[m + bit], "grp", bit)
            for m in reversed(range(2 * bit, groups, 2 * bit))
        }
        slots = {0: slots[0] + swap(slots[bit], "grp", bit), **ahead}
        bit *= 2
    maps = gather_pairs(step)
    others = [
        swap(jnp.concatenate(pair, axis=0), "leaf", 1) for pair in (maps[:-1], maps[-1:]) if pair
    ]
    offset = own - slots[0]
    offsets = gather_pairs(offset[None])
    rows = call(
        operator_rows, shaped(sections, 2 * order, order), 4 * sections * cube,
        4 * sections * block_bytes, *maps, *others,
        held=[pltpu.VMEM((sections, order, order), F32)],
    )

    base, factors = call(
        leaf_base,
        (shaped(count, order, columns), jax.ShapeDtypeStruct((count * order, 3 * order), BF16)),
        (groups + 1) * count * cube, 3 * leaf_rhs.size * 4, leaf_rhs, leaf_inv, down,
    )

    def applied(which, order_only):
        return call(
            lambda *refs: apply_rows(which, *refs), block, *placed, rows, order_only, *offsets,
        )

    theirs = swap(applied(1, down), "leaf", 1)
    carried = applied(0, factors) + theirs
    spread, slots, bit = carried[None], [0], groups // 2
    while bit > 1:
        spread = jnp.concatenate([spread, swap(spread, "grp", bit)], axis=0)
        slots = slots + [slot ^ bit for slot in slots]
        bit //= 2
    late = [slot ^ 1 for slot in slots]
    arrived = swap(spread, "grp", 1)
    done, solved = call(
        lambda *refs: early_blocks(slots, *refs),
        (shaped(len(slots), count, order, width), shaped(1, order, width)),
        (len(slots) * count + 1) * cube, 4 * leaf_rhs.size, base, factors, sep_inv, spread,
    )
    leaves = call(
        lambda *refs: late_blocks(slots, late, *refs), shaped(1, count, order, columns),
        len(late) * count * cube, 8 * leaf_rhs.size, base, factors, arrived, done,
        held=[
            pltpu.VMEM((len(late), count, order, width), F32),
            pltpu.SemaphoreType.DMA((groups,)),
        ],
        out_specs=HBM,
    )
    return leaves, solved


def solution(mesh):
    in_specs = (
        P("leaf", "grp", None, None),
        P("leaf", "grp", None, None),
        P("leaf", "grp", None, None),
        P("leaf", "grp"),
        P("leaf", None, None),
        P("leaf", None, None),
        P("leaf", None, None),
    )
    out_specs = (P("leaf", "grp", None, None), P("leaf", None, "grp"))
    return jax.shard_map(shards, mesh=mesh, in_specs=in_specs, out_specs=out_specs, check_vma=False)
```

```python
import jax
import jax.numpy as jnp
from jax import lax
from jax.experimental import pallas as pl
from jax.experimental.pallas import tpu as pltpu
from jax.sharding import PartitionSpec as P

HIGH = lax.Precision.HIGHEST
F32 = jnp.float32
BF16 = jnp.bfloat16
VMEM = pl.BlockSpec(memory_space=pltpu.VMEM)
HBM = pl.BlockSpec(memory_space=pltpu.HBM)


def dot(a, b):
    return jnp.dot(a, b, precision=HIGH, preferred_element_type=F32)


def dot_ta(a, b):
    return lax.dot_general(
        a, b, (((0,), (0,)), ((), ())), precision=HIGH, preferred_element_type=F32
    )


def split(x):
    high = x.astype(BF16)
    return high, (x - high.astype(F32)).astype(BF16)


def left(x):
    high, low = split(x)
    return jnp.concatenate([high, low, high], axis=1)


def right(x, axis=0):
    high, low = split(x)
    return jnp.concatenate([high, high, low], axis=axis)


def dot3(a, b):
    return jnp.dot(left(a), right(b), preferred_element_type=F32)


def dot3_tb(a, b):
    return lax.dot_general(
        left(a), right(b, 1), (((1,), (1,)), ((), ())), preferred_element_type=F32
    )


def shaped(*shape):
    return jax.ShapeDtypeStruct(shape, F32)


def call(body, outs, flops, moved, *args, held=(), far=0, out_specs=None):
    args = [pltpu.with_memory_space_constraint(a, pltpu.HBM) for a in args[:far]] + list(args[far:])
    return pl.pallas_call(
        body,
        out_shape=outs,
        in_specs=[HBM] * far + [VMEM] * (len(args) - far),
        out_specs=out_specs or jax.tree.map(lambda _: VMEM, outs),
        scratch_shapes=held,
        cost_estimate=pl.CostEstimate(flops=flops, bytes_accessed=moved, transcendentals=0),
        compiler_params=pltpu.CompilerParams(vmem_limit_bytes=48 << 20),
    )(*args)


def landing(*args):
    holds = [
        (pltpu.SMEM if a.dtype == jnp.int32 else pltpu.VMEM)(a.shape, a.dtype) for a in args
    ]
    return holds + [pltpu.SemaphoreType.DMA((len(args),))]


def fetch(sources, targets, sems):
    copies = [
        pltpu.make_async_copy(a, b, sems.at[i]) for i, (a, b) in enumerate(zip(sources, targets))
    ]
    for copy in copies:
        copy.start()
    return copies


def columns_of(block, width):
    return pl.ds(pl.multiple_of(block * width, width), width)


def begin(*refs):
    sources, outs = refs[:5], refs[5:-6]
    down, slots = outs[0], outs[1:]
    targets, sems = refs[-6:-1], refs[-1]
    inverse, pattern, leaf_inv, coupling, rhs = targets
    copies = fetch(sources, targets, sems)
    group = lax.axis_index("grp")
    count, width = down.shape[0], slots[0].shape[1]
    for copy in copies[:4]:
        copy.wait()
    for k in range(count):
        present = pattern[0, k].astype(F32)
        mixed = dot3(coupling[0, k] * present, leaf_inv[0, k])
        down[k] = dot3(inverse[0], mixed)
    copies[4].wait()
    joined = left(jnp.concatenate([down[k] for k in range(count)], axis=1))
    for first in reversed(range(0, len(slots), 2)):
        pair = [columns_of(group ^ slot, width) for slot in range(first, first + 2)]
        stacked = jnp.concatenate(
            [jnp.concatenate([rhs[0, k, :, cols] for cols in pair], axis=1) for k in range(count)],
            axis=0,
        )
        total = jnp.dot(joined, right(stacked), preferred_element_type=F32)
        slots[first][...] = total[:, :width]
        slots[first + 1][...] = total[:, width:]


def section_map(inverse, link, order_only, out):
    out[0] = -dot(inverse[0], link[0])


def leaf_base(rhs, leaf_inv, down, base, factors):
    order = down.shape[1]
    for k in range(base.shape[0]):
        gram = dot_ta(leaf_inv[0, k], leaf_inv[0, k])
        base[k] = dot(gram, rhs[0, k])
        factors[k * order : (k + 1) * order] = left(down[k].T)


def own_columns(rhs, inverse, out):
    out[...] = dot(inverse[0], rhs[0, :, columns_of(lax.axis_index("grp"), out.shape[1])])


def operator_rows(*refs):
    parts, (held, maps) = refs[:-2], refs[-2:]
    sections, both, order = held.shape
    me = lax.axis_index("leaf")
    at = 0
    for part in parts:
        size, begun = part.shape[0], at

        @pl.loop(0, size, unroll=size <= 8)
        def _(i):
            spot = i + begun
            maps[(2 * spot if begun < sections // 2 else 2 * spot + 1 - sections) ^ me] = part[i]

        at += size

    line = lax.broadcasted_iota(jnp.int32, (both, order), 0)
    column = lax.broadcasted_iota(jnp.int32, (both, order), 1)
    target = jnp.where(line < order, me, me ^ 1)
    ones = jnp.where((line & (order - 1)) == column, target, -1)

    held[0] = (ones == 0).astype(F32)

    @pl.loop(1, sections, unroll=sections <= 8)
    def _(section):
        held[section] = dot3_tb(held[section - 1], maps[section]) + (ones == section).astype(F32)

    @pl.loop(0, sections - 1, unroll=sections <= 8)
    def _(turn):
        section = sections - 2 - turn
        held[section] += dot3(held[section + 1], maps[section + 1])


def apply_rows(which, held, order_only, *refs):
    parts, out = refs[:-1], refs[-1]
    order = held.shape[2]
    rows = slice(which * order, (which + 1) * order)
    me = lax.axis_index("leaf")
    size = parts[0].shape[0]
    total = None
    for p, part in enumerate(parts):
        for i in range(size):
            piece = dot3(held[2 * (p * size + i) ^ me, rows], part[i])
            total = piece if total is None else total + piece
    out[...] = total


def leaf_blocks(slots, base, factors, spread, out):
    count, order = base.shape[:2]
    width = spread.shape[2]
    for first in range(0, len(slots), 2):
        ready = range(first, min(first + 2, len(slots)))
        stacked = jnp.concatenate([spread[i] for i in ready], axis=1)
        taken = jnp.dot(factors[...], right(stacked), preferred_element_type=F32)
        for i in ready:
            cols = columns_of(lax.axis_index("grp") ^ slots[i], width)
            near = slice((i - first) * width, (i - first + 1) * width)
            for k in range(count):
                out[i, k] = base[k, :, cols] - taken[k * order : (k + 1) * order, near]


def early_blocks(slots, base, factors, inverse, spread, out, solved):
    leaf_blocks(slots, base, factors, spread, out)
    solved[0] = dot_ta(inverse[0], spread[0])


def late_blocks(early, late, base, factors, spread, *refs):
    done, (leaves, fresh, sems) = refs[:-3], refs[-3:]
    width = spread.shape[2]

    def put(slot, source):
        target = leaves.at[0, :, :, columns_of(lax.axis_index("grp") ^ slot, width)]
        return pltpu.make_async_copy(source, target, sems.at[slot])

    copies = [
        put(slot, blocks.at[i]) for slots, blocks in zip(early, done) for i, slot in enumerate(slots)
    ]
    for copy in copies:
        copy.start()
    leaf_blocks([late], base, factors, spread, fresh)
    copies.append(put(late, fresh.at[0]))
    copies[-1].start()
    for copy in copies:
        copy.wait()


def swap(value, axis, bit):
    count = lax.axis_size(axis)
    return lax.ppermute(value, axis, [(i, i ^ bit) for i in range(count)])


def gather_pairs(value):
    bit, sections = 2, lax.axis_size("leaf")
    parts = [value]
    while bit < sections:
        if len(parts) > 1:
            value = jnp.concatenate(parts, axis=0)
        masks = [bit] if 2 * bit >= sections else [bit, 2 * bit, 3 * bit]
        parts = [value] + [swap(value, "leaf", m) for m in masks]
        bit *= 4 if len(masks) > 1 else 2
    return parts


def shards(leaf_rhs, leaf_inv, coupling, pattern, sep_rhs, sep_inv, chain_link):
    sections, groups = lax.axis_size("leaf"), lax.axis_size("grp")
    count, order, columns = leaf_rhs.shape[1:]
    width = columns // groups
    cube = 2 * order**3
    block = shaped(order, width)
    block_bytes = order * width * 4
    placed = (40 * sections * cube, 60 << 20)

    first = (sep_inv, pattern, leaf_inv, coupling, leaf_rhs)
    down, *slots = call(
        begin,
        (shaped(count, order, order),) + (block,) * groups,
        *placed,
        *first, held=landing(*first), far=5,
    )
    step = call(
        section_map, shaped(1, order, order), *placed,
        sep_inv, chain_link, down,
    )
    slots = dict(enumerate(slots))
    own = call(own_columns, block, *placed, sep_rhs, sep_inv)
    bit = 1
    while bit < groups:
        ahead = {
            m: slots[m] + swap(slots[m + bit], "grp", bit)
            for m in reversed(range(2 * bit, groups, 2 * bit))
        }
        slots = {0: slots[0] + swap(slots[bit], "grp", bit), **ahead}
        bit *= 2
    maps = gather_pairs(step)
    others = [
        swap(jnp.concatenate(pair, axis=0), "leaf", 1) for pair in (maps[:-1], maps[-1:]) if pair
    ]
    offset = own - slots[0]
    offsets = gather_pairs(offset[None])
    rows = call(
        operator_rows, shaped(sections, 2 * order, order), 4 * sections * cube,
        4 * sections * block_bytes, *maps, *others,
        held=[pltpu.VMEM((sections, order, order), F32)],
    )

    base, factors = call(
        leaf_base,
        (shaped(count, order, columns), jax.ShapeDtypeStruct((count * order, 3 * order), BF16)),
        (groups + 1) * count * cube, 3 * leaf_rhs.size * 4, leaf_rhs, leaf_inv, down,
    )

    def applied(which, order_only):
        return call(
            lambda *refs: apply_rows(which, *refs), block, *placed, rows, order_only, *offsets,
        )

    theirs = swap(applied(1, down), "leaf", 1)
    carried = applied(0, factors) + theirs
    blocks = {0: carried[None]}
    for m in sorted(range(1, groups), key=lambda m: (m & (m - 1) != 0, -m)):
        blocks[m] = swap(blocks[m & (m - 1)], "grp", m & -m)
    early, solved = call(
        lambda *refs: early_blocks([0, 1], *refs),
        (shaped(2, count, order, width), shaped(1, order, width)),
        (2 * count + 1) * cube, 4 * leaf_rhs.size, base, factors, sep_inv, jnp.concatenate([blocks[0], blocks[1]], axis=0),
    )
    done, slots = [early], [[0, 1]]
    for m in range(2, groups - 1):
        slots.append([m])
        done.append(
            call(
                lambda *refs, m=m: leaf_blocks([m], *refs), shaped(1, count, order, width),
                count * cube, 2 * leaf_rhs.size, base, factors, blocks[m],
            )
        )
    leaves = call(
        lambda *refs: late_blocks(slots, groups - 1, *refs), shaped(1, count, order, columns),
        count * cube, 8 * leaf_rhs.size, base, factors, blocks[groups - 1], *done,
        held=[pltpu.VMEM((1, count, order, width), F32), pltpu.SemaphoreType.DMA((groups,))],
        out_specs=HBM,
    )
    return leaves, solved


def solution(mesh):
    in_specs = (
        P("leaf", "grp", None, None),
        P("leaf", "grp", None, None),
        P("leaf", "grp", None, None),
        P("leaf", "grp"),
        P("leaf", None, None),
        P("leaf", None, None),
        P("leaf", None, None),
    )
    out_specs = (P("leaf", "grp", None, None), P("leaf", None, "grp"))
    return jax.shard_map(shards, mesh=mesh, in_specs=in_specs, out_specs=out_specs, check_vma=False)
```

```python
import jax
import jax.numpy as jnp
from jax import lax
from jax.experimental import pallas as pl
from jax.experimental.pallas import tpu as pltpu
from jax.sharding import PartitionSpec as P

HIGH = lax.Precision.HIGHEST
F32 = jnp.float32
BF16 = jnp.bfloat16
VMEM = pl.BlockSpec(memory_space=pltpu.VMEM)
HBM = pl.BlockSpec(memory_space=pltpu.HBM)


def dot(a, b):
    return jnp.dot(a, b, precision=HIGH, preferred_element_type=F32)


def dot_ta(a, b):
    return lax.dot_general(
        a, b, (((0,), (0,)), ((), ())), precision=HIGH, preferred_element_type=F32
    )


def split(x):
    high = x.astype(BF16)
    return high, (x - high.astype(F32)).astype(BF16)


def left(x):
    high, low = split(x)
    return jnp.concatenate([high, low, high], axis=1)


def right(x, axis=0):
    high, low = split(x)
    return jnp.concatenate([high, high, low], axis=axis)


def dot3(a, b):
    return jnp.dot(left(a), right(b), preferred_element_type=F32)


def dot3_tb(a, b):
    return lax.dot_general(
        left(a), right(b, 1), (((1,), (1,)), ((), ())), preferred_element_type=F32
    )


def shaped(*shape):
    return jax.ShapeDtypeStruct(shape, F32)


def call(body, outs, flops, moved, *args, held=(), far=0, out_specs=None):
    args = [pltpu.with_memory_space_constraint(a, pltpu.HBM) for a in args[:far]] + list(args[far:])
    return pl.pallas_call(
        body,
        out_shape=outs,
        in_specs=[HBM] * far + [VMEM] * (len(args) - far),
        out_specs=out_specs or jax.tree.map(lambda _: VMEM, outs),
        scratch_shapes=held,
        cost_estimate=pl.CostEstimate(flops=flops, bytes_accessed=moved, transcendentals=0),
        compiler_params=pltpu.CompilerParams(vmem_limit_bytes=48 << 20),
    )(*args)


def landing(*args):
    holds = [
        (pltpu.SMEM if a.dtype == jnp.int32 else pltpu.VMEM)(a.shape, a.dtype) for a in args
    ]
    return holds + [pltpu.SemaphoreType.DMA((len(args),))]


def fetch(sources, targets, sems):
    copies = [
        pltpu.make_async_copy(a, b, sems.at[i]) for i, (a, b) in enumerate(zip(sources, targets))
    ]
    for copy in copies:
        copy.start()
    return copies


def columns_of(block, width):
    return pl.ds(pl.multiple_of(block * width, width), width)


def begin(*refs):
    sources, outs = refs[:5], refs[5:-6]
    down, slots = outs[0], outs[1:]
    targets, sems = refs[-6:-1], refs[-1]
    inverse, pattern, leaf_inv, coupling, rhs = targets
    copies = fetch(sources, targets, sems)
    group = lax.axis_index("grp")
    count, width = down.shape[0], slots[0].shape[1]
    for copy in copies[:4]:
        copy.wait()
    for k in range(count):
        present = pattern[0, k].astype(F32)
        mixed = dot3(coupling[0, k] * present, leaf_inv[0, k])
        down[k] = dot3(inverse[0], mixed)
    copies[4].wait()
    joined = left(jnp.concatenate([down[k] for k in range(count)], axis=1))
    for first in reversed(range(0, len(slots), 2)):
        pair = [columns_of(group ^ slot, width) for slot in range(first, first + 2)]
        stacked = jnp.concatenate(
            [jnp.concatenate([rhs[0, k, :, cols] for cols in pair], axis=1) for k in range(count)],
            axis=0,
        )
        total = jnp.dot(joined, right(stacked), preferred_element_type=F32)
        slots[first][...] = total[:, :width]
        slots[first + 1][...] = total[:, width:]


def section_map(inverse, link, order_only, out):
    out[0] = -dot3(inverse[0], link[0])


def leaf_base(rhs, leaf_inv, down, base, factors):
    order = down.shape[1]
    for k in range(base.shape[0]):
        gram = dot_ta(leaf_inv[0, k], leaf_inv[0, k])
        base[k] = dot3(gram, rhs[0, k])
        factors[k * order : (k + 1) * order] = left(down[k].T)


def own_columns(rhs, inverse, out):
    out[...] = dot3(inverse[0], rhs[0, :, columns_of(lax.axis_index("grp"), out.shape[1])])


def operator_rows(*refs):
    parts, (held, maps) = refs[:-2], refs[-2:]
    sections, both, order = held.shape
    me = lax.axis_index("leaf")
    at = 0
    for part in parts:
        size, begun = part.shape[0], at

        @pl.loop(0, size, unroll=size <= 8)
        def _(i):
            spot = i + begun
            maps[(2 * spot if begun < sections // 2 else 2 * spot + 1 - sections) ^ me] = part[i]

        at += size

    line = lax.broadcasted_iota(jnp.int32, (both, order), 0)
    column = lax.broadcasted_iota(jnp.int32, (both, order), 1)
    target = jnp.where(line < order, me, me ^ 1)
    ones = jnp.where((line & (order - 1)) == column, target, -1)

    held[0] = (ones == 0).astype(F32)

    @pl.loop(1, sections, unroll=sections <= 8)
    def _(section):
        held[section] = dot3_tb(held[section - 1], maps[section]) + (ones == section).astype(F32)

    @pl.loop(0, sections - 1, unroll=sections <= 8)
    def _(turn):
        section = sections - 2 - turn
        held[section] += dot3(held[section + 1], maps[section + 1])


def apply_rows(which, held, order_only, *refs):
    parts, out = refs[:-1], refs[-1]
    order = held.shape[2]
    rows = slice(which * order, (which + 1) * order)
    me = lax.axis_index("leaf")
    size = parts[0].shape[0]
    total = None
    for p, part in enumerate(parts):
        for i in range(size):
            piece = dot3(held[2 * (p * size + i) ^ me, rows], part[i])
            total = piece if total is None else total + piece
    out[...] = total


def leaf_blocks(slots, base, factors, spread, out):
    count, order = base.shape[:2]
    width = spread.shape[2]
    for first in range(0, len(slots), 2):
        ready = range(first, min(first + 2, len(slots)))
        stacked = jnp.concatenate([spread[i] for i in ready], axis=1)
        taken = jnp.dot(factors[...], right(stacked), preferred_element_type=F32)
        for i in ready:
            cols = columns_of(lax.axis_index("grp") ^ slots[i], width)
            near = slice((i - first) * width, (i - first + 1) * width)
            for k in range(count):
                out[i, k] = base[k, :, cols] - taken[k * order : (k + 1) * order, near]


def early_blocks(slots, base, factors, inverse, spread, out, solved):
    leaf_blocks(slots, base, factors, spread, out)
    solved[0] = dot_ta(inverse[0], spread[0])


def late_blocks(early, late, base, factors, spread, *refs):
    done, (leaves, fresh, sems) = refs[:-3], refs[-3:]
    width = spread.shape[2]

    def put(slot, source):
        target = leaves.at[0, :, :, columns_of(lax.axis_index("grp") ^ slot, width)]
        return pltpu.make_async_copy(source, target, sems.at[slot])

    copies = [
        put(slot, blocks.at[i]) for slots, blocks in zip(early, done) for i, slot in enumerate(slots)
    ]
    for copy in copies:
        copy.start()
    leaf_blocks([late], base, factors, spread, fresh)
    copies.append(put(late, fresh.at[0]))
    copies[-1].start()
    for copy in copies:
        copy.wait()


def swap(value, axis, bit):
    count = lax.axis_size(axis)
    return lax.ppermute(value, axis, [(i, i ^ bit) for i in range(count)])


def gather_pairs(value):
    bit, sections = 2, lax.axis_size("leaf")
    parts = [value]
    while bit < sections:
        if len(parts) > 1:
            value = jnp.concatenate(parts, axis=0)
        masks = [bit] if 2 * bit >= sections else [bit, 2 * bit, 3 * bit]
        parts = [value] + [swap(value, "leaf", m) for m in masks]
        bit *= 4 if len(masks) > 1 else 2
    return parts


def shards(leaf_rhs, leaf_inv, coupling, pattern, sep_rhs, sep_inv, chain_link):
    sections, groups = lax.axis_size("leaf"), lax.axis_size("grp")
    count, order, columns = leaf_rhs.shape[1:]
    width = columns // groups
    cube = 2 * order**3
    block = shaped(order, width)
    block_bytes = order * width * 4
    placed = (40 * sections * cube, 60 << 20)

    first = (sep_inv, pattern, leaf_inv, coupling, leaf_rhs)
    down, *slots = call(
        begin,
        (shaped(count, order, order),) + (block,) * groups,
        *placed,
        *first, held=landing(*first), far=5,
    )
    step = call(
        section_map, shaped(1, order, order), *placed,
        sep_inv, chain_link, down,
    )
    slots = dict(enumerate(slots))
    own = call(own_columns, block, *placed, sep_rhs, sep_inv)
    bit = 1
    while bit < groups:
        ahead = {
            m: slots[m] + swap(slots[m + bit], "grp", bit)
            for m in reversed(range(2 * bit, groups, 2 * bit))
        }
        slots = {0: slots[0] + swap(slots[bit], "grp", bit), **ahead}
        bit *= 2
    maps = gather_pairs(step)
    others = [
        swap(jnp.concatenate(pair, axis=0), "leaf", 1) for pair in (maps[:-1], maps[-1:]) if pair
    ]
    offset = own - slots[0]
    offsets = gather_pairs(offset[None])
    rows = call(
        operator_rows, shaped(sections, 2 * order, order), 4 * sections * cube,
        4 * sections * block_bytes, *maps, *others,
        held=[pltpu.VMEM((sections, order, order), F32)],
    )

    base, factors = call(
        leaf_base,
        (shaped(count, order, columns), jax.ShapeDtypeStruct((count * order, 3 * order), BF16)),
        (groups + 1) * count * cube, 3 * leaf_rhs.size * 4, leaf_rhs, leaf_inv, down,
    )

    def applied(which, order_only):
        return call(
            lambda *refs: apply_rows(which, *refs), block, *placed, rows, order_only, *offsets,
        )

    theirs = swap(applied(1, down), "leaf", 1)
    carried = applied(0, factors) + theirs
    blocks = {0: carried[None]}
    for m in sorted(range(1, groups), key=lambda m: (m & (m - 1) != 0, -m)):
        blocks[m] = swap(blocks[m & (m - 1)], "grp", m & -m)
    early, solved = call(
        lambda *refs: early_blocks([0, 1], *refs),
        (shaped(2, count, order, width), shaped(1, order, width)),
        (2 * count + 1) * cube, 4 * leaf_rhs.size, base, factors, sep_inv, jnp.concatenate([blocks[0], blocks[1]], axis=0),
    )
    done, slots = [early], [[0, 1]]
    for m in range(2, groups - 1):
        slots.append([m])
        done.append(
            call(
                lambda *refs, m=m: leaf_blocks([m], *refs), shaped(1, count, order, width),
                count * cube, 2 * leaf_rhs.size, base, factors, blocks[m],
            )
        )
    leaves = call(
        lambda *refs: late_blocks(slots, groups - 1, *refs), shaped(1, count, order, columns),
        count * cube, 8 * leaf_rhs.size, base, factors, blocks[groups - 1], *done,
        held=[pltpu.VMEM((1, count, order, width), F32), pltpu.SemaphoreType.DMA((groups,))],
        out_specs=HBM,
    )
    return leaves, solved


def solution(mesh):
    in_specs = (
        P("leaf", "grp", None, None),
        P("leaf", "grp", None, None),
        P("leaf", "grp", None, None),
        P("leaf", "grp"),
        P("leaf", None, None),
        P("leaf", None, None),
        P("leaf", None, None),
    )
    out_specs = (P("leaf", "grp", None, None), P("leaf", None, "grp"))
    return jax.shard_map(shards, mesh=mesh, in_specs=in_specs, out_specs=out_specs, check_vma=False)
```
